256 devices in a mesh: wide: 16 (over y_hi, z), narrow: 16 (over y_lo, x, core).
Axes of the slice: x: 4, y: 4 (y_hi: 2, y_lo: 2; y = y_hi * 2 + y_lo), z: 8, core: 2. Of those that a mesh axis runs over, the one named last changes fastest.
Arguments:
- quantized_inputs: bfloat16 [16384, 3072], P(('wide', 'narrow')), may hold values from -6 to 6
- x_full: bfloat16 [16384, 3072], P(('wide', 'narrow')), may hold values from -6 to 6
Outputs:
- gram_out: float32 [16, 16, 64, 16384], P(None, 'narrow', None, 'wide')
- cross_gram_result: float32 [16, 16, 64, 16384], P(None, 'narrow', None, 'wide')
The draws below stay inside these ranges and needn't reach their ends.
All inputs are finite; a program needn't handle non-finite values.
Results may differ from the reference program's by a relative error of at most 0.003.
Values may be sent and summed in bfloat16 or wider, within the bound.
A program may use at most 128 MiB of HBM per device.

```python
import jax
import jax.numpy as jnp

D = 16384
TOKENS = 3072
WIDE_DEVS = 16
NARROW_DEVS = 16
FD = 64


def block_scale(own_key, shape, shards, smallest, top_value):
    level = 1.0
    for axis_at, shards_of in shards:
        heights = jax.random.uniform(jax.random.fold_in(jax.random.fold_in(own_key, 6), axis_at), (shards_of,), jnp.float32, smallest / len(shards), top_value / len(shards))
        level = level * jnp.repeat(jnp.exp(heights), shape[axis_at] // shards_of).reshape((-1,) + (1,) * (len(shape) - 1 - axis_at))
    return level


def scatter_about(own_key, extent, deviation, bound, shards=(), dtype=jnp.bfloat16):
    result = jax.random.normal(own_key, extent, jnp.float32) * deviation
    if len(shards) > 0:
        result = block_scale(own_key, extent, shards, -0.22, 0.18) * result
    return jnp.clip(result, min=-bound, max=bound).astype(dtype)


def setup_inputs(seed: int = 0) -> dict:
    keys = jax.random.split(jax.random.key(seed), 3)
    return {
        "quantized_inputs": scatter_about(keys[0], (D, TOKENS), 1.0, 6.0, ((0, 256),)),
        "x_full": scatter_about(keys[1], (D, TOKENS), 1.0, 6.0, ((0, 256),)),
    }


def reference(quantized_inputs, x_full):
    difference = (x_full.astype(jnp.float32) - quantized_inputs.astype(jnp.float32)).astype(jnp.bfloat16)
    complete_gram = jnp.dot(quantized_inputs, quantized_inputs.T, preferred_element_type=jnp.float32) / TOKENS
    cross_whole = jnp.dot(difference, quantized_inputs.T, preferred_element_type=jnp.float32) / TOKENS
    gram_out = complete_gram.reshape(WIDE_DEVS, NARROW_DEVS, FD, D)
    cross_gram_result = cross_whole.reshape(WIDE_DEVS, NARROW_DEVS, FD, D)
    return gram_out, cross_gram_result
```

```python
import heapq

import jax
import jax.numpy as jnp
from jax import lax
from jax.experimental import pallas as pl
from jax.experimental.pallas import tpu as pltpu
from jax.sharding import PartitionSpec as P

MESH = pl.DeviceIdType.MESH
BF16 = jnp.bfloat16
F32 = jnp.float32

NZ, NX = 8, 4
Z_OFFSET = (0, -1, 1, -2, 2, -3, 3, 4)
GROUPS = ((0, 1), (1, 2), (3, 2), (5, 2), (7, 1))
OPP, OWN = 0, 1
STEP_US = 8.46


class Messages:
    def __init__(self, send_sem, recv_sem):
        self.send_sem, self.recv_sem = send_sem, recv_sem
        self.copies = []

    def make(self, src, dst, device):
        i = len(self.copies)
        copy = pltpu.make_async_remote_copy(
            src_ref=src,
            dst_ref=dst,
            send_sem=self.send_sem.at[i],
            recv_sem=self.recv_sem.at[i],
            device_id=device,
            device_id_type=MESH,
        )
        self.copies.append(copy)
        return copy


def out_times(produced):
    queue, free, landed, n = [], 0.0, {}, 0
    for tile, (at, blocks) in produced.items():
        heapq.heappush(queue, (at, n, 0, tile, blocks))
        n += 1
    while queue:
        at, _, hop, tile, blocks = heapq.heappop(queue)
        free = max(free, at) + 0.0835 * blocks
        if hop == 0:
            landed[tile] = free + 0.12
            heapq.heappush(queue, (free + 0.12, n, 1, tile, blocks))
            n += 1
    return landed


N_SEND = 14 + 12 + 4 + 16 + 40 + 64


def kernel(q_in, x_in, out, left, xs_left, right, ship, relay, own_out, send_sem, recv_sem, local_sem):
    tokens = q_in.shape[1]
    fd = q_in.shape[0]
    scale = 1.0 / tokens
    wide, narrow = lax.axis_index("wide"), lax.axis_index("narrow")
    yh, z = wide // NZ, wide % NZ
    yl, x, core = narrow // (2 * NX), (narrow // 2) % NX, narrow % 2

    def device(yh_, z_, yl_, x_, core_):
        return (yh_ * NZ + z_, (yl_ * NX + x_) * 2 + core_)

    z_up, z_down = (device(yh, (z + d) % NZ, yl, x, core) for d in (1, NZ - 1))
    x_up, x_down = (device(yh, z, yl, (x + d) % NX, core) for d in (1, NX - 1))
    partner = device(yh, z, yl, x, 1 - core)
    y_opp = device(1 - yh, z, 1 - yl, x, core)
    y_own = device(yh, z, 1 - yl, x, core)

    barrier = pltpu.get_barrier_semaphore()
    neighbours = (z_up, z_down, x_up, x_down, partner, y_opp, y_own)
    for d in neighbours:
        pl.semaphore_signal(barrier, inc=1, device_id=d, device_id_type=MESH)
    pl.semaphore_wait(barrier, len(neighbours))

    messages = Messages(send_sem, recv_sem)
    make = messages.make
    waited = set()

    def need(copy):
        if id(copy) not in waited:
            waited.add(id(copy))
            copy.wait_recv()

    locals_ = [
        pltpu.make_async_copy(q_in, left.at[0, 0], local_sem.at[0]),
        pltpu.make_async_copy(x_in, xs_left.at[0], local_sem.at[1]),
        pltpu.make_async_copy(q_in, right.at[1, OWN, 0, core], local_sem.at[2]),
    ]

    z_msgs = {}
    for up in (True, False):
        to = z_up if up else z_down
        for k in (1, 2, 3, 4):
            src_slot = 0 if k == 1 else (2 * (k - 1) - 1 if up else 2 * (k - 1))
            dst_slot = 7 if k == 4 else (2 * k - 1 if up else 2 * k)
            if k < 4 or up:
                src = q_in if k == 1 else left.at[src_slot, 0]
                z_msgs[up, k, "q"] = make(src, left.at[dst_slot, 0], to)
            if k < 4 or not up:
                src = x_in if k == 1 else xs_left.at[src_slot]
                z_msgs[up, k, "x"] = make(src, xs_left.at[dst_slot], to)

    def left_messages(slot):
        if slot == 0:
            return []
        if slot == 7:
            return [z_msgs[True, 4, "q"], z_msgs[False, 4, "x"]]
        up, k = slot % 2 == 1, (slot + 1) // 2
        return [z_msgs[up, k, "q"], z_msgs[up, k, "x"]]

    half = fd // 2
    lo, hi = pl.ds(0, half), pl.ds(half, half)
    y_to_opp = make(q_in, right.at[1, OPP, 1, core], y_opp)
    y_to_own = make(q_in, right.at[1, OWN, 1, core], y_own)
    y_two_a = make(right.at[1, OPP, 1, core, lo], right.at[1, OPP, 0, core, lo], y_own)
    y_two_b = make(right.at[1, OWN, 1, core, hi], right.at[1, OPP, 0, core, hi], y_opp)

    x_msgs = {}
    for hy in (OPP, OWN):
        for ly in (0, 1):
            src = q_in if (hy, ly) == (OWN, 0) else right.at[1, hy, ly, core]
            x_msgs["up", hy, ly] = make(src, right.at[0, hy, ly, core], x_up)
            x_msgs["down", hy, ly] = make(src, right.at[2, hy, ly, core], x_down)
    for hy, ly in ((OPP, 1), (OWN, 0)):
        x_msgs["far", hy, ly] = make(right.at[0, hy, ly, core], right.at[3, hy, ly, core], x_up)
    for hy, ly in ((OPP, 0), (OWN, 1)):
        x_msgs["far", hy, ly] = make(right.at[2, hy, ly, core], right.at[3, hy, ly, core], x_down)

    p_msgs = {}
    for xs in range(4):
        for hy in (OPP, OWN):
            for ly in (0, 1):
                src = q_in if (xs, hy, ly) == (1, OWN, 0) else right.at[xs, hy, ly, core]
                p_msgs[xs, hy, ly] = make(src, right.at[xs, hy, ly, core], partner)

    x_way = {0: "up", 2: "down", 3: "far"}

    def right_messages(xs, hy):
        got = [p_msgs[xs, hy, ly] for ly in (0, 1)]
        if xs != 1:
            return [x_msgs[x_way[xs], hy, ly] for ly in (0, 1)] + got
        if hy == OPP:
            return [y_to_opp, y_two_a, y_two_b] + got
        return [y_to_own] + got

    first, second = {}, {}
    for g, (l0, nl) in enumerate(GROUPS):
        for xs in range(4):
            for path in (0, 1):
                rows = pl.ds(l0, nl)
                first[g, xs, path] = make(
                    ship.at[path, xs, rows], relay.at[path, xs, rows], (y_opp, y_own)[path]
                )
                src_yh = 1 - yh if path == 0 else yh
                col_yl = 1 - yl if path == 0 else yl
                col = pl.multiple_of(col_yl * (2 * NX * fd) + ((x + xs + NX - 1) % NX) * (2 * fd), 2 * fd)
                second[g, xs, path] = [
                    make(
                        relay.at[path, xs, l],
                        out.at[:, src_yh * NZ + (z + Z_OFFSET[l] + NZ) % NZ, :, pl.ds(col, 2 * fd)],
                        (y_own, y_opp)[path],
                    )
                    for l in range(l0, l0 + nl)
                ]
    assert len(messages.copies) == N_SEND, len(messages.copies)

    have_diff = set()

    def diff(slot):
        if slot in have_diff:
            return
        have_diff.add(slot)
        if slot == 0:
            locals_[0].wait()
            locals_[1].wait()
        for m in left_messages(slot):
            need(m)
        left[slot, 1] = (xs_left[slot].astype(F32) - left[slot, 0].astype(F32)).astype(BF16)

    have_own = []

    def ready(g, xs_list, hy):
        l0, nl = GROUPS[g]
        for slot in range(l0, l0 + nl):
            diff(slot)
        for xs in xs_list:
            if (xs, hy) == (1, OWN) and not have_own:
                have_own.append(1)
                locals_[2].wait()
            for m in right_messages(xs, hy):
                need(m)

    def product(l0, nl, xs, hy):
        a = left[pl.ds(l0, nl)].reshape(nl * 2 * fd, tokens)
        b = right[xs, hy].reshape(4 * fd, tokens)
        p = lax.dot_general(a, b, (((1,), (1,)), ((), ())), preferred_element_type=F32) * scale
        return p.astype(BF16).reshape(nl, 2, fd, 4 * fd)

    def opp_tile(g, xs):
        l0, nl = GROUPS[g]
        p = product(l0, nl, xs, OPP)
        for path in (0, 1):
            ship[path, xs, l0 : l0 + nl] = p[..., path * 2 * fd : (path + 1) * 2 * fd]

    def own_tiles(g, start, step, count):
        l0, nl = GROUPS[g]

        def one(i, _):
            xs = start + i * step
            p = product(l0, nl, xs, OWN)
            for ly in (0, 1):
                col_yl = yl if ly == 0 else 1 - yl
                col = pl.multiple_of(col_yl * (2 * NX * fd) + ((x + xs + NX - 1) % NX) * (2 * fd), 2 * fd)
                own_out[l0 : l0 + nl, :, :, pl.ds(col, 2 * fd)] = p[..., ly * 2 * fd : (ly + 1) * 2 * fd]
            return 0

        if count == 1:
            one(0, 0)
        else:
            lax.fori_loop(0, count, one, 0)

    events = []

    def at(time, fn):
        events.append((time, len(events), fn))

    def forward_z(what, k):
        def go():
            for up in (True, False):
                if (up, k, what) in z_msgs:
                    need(z_msgs[up, k, what])
                if (up, k + 1, what) in z_msgs:
                    z_msgs[up, k + 1, what].start()

        return go

    for k in (1, 2, 3):
        at(2 * k - 1 + 0.02, forward_z("q", k))
        at(2 * k + 0.02, forward_z("x", k))

    def start_all():
        for key in ((True, 1, "q"), (False, 1, "q")):
            z_msgs[key].start()
        y_to_opp.start()
        y_to_own.start()
        x_msgs["up", OWN, 0].start()
        x_msgs["down", OWN, 0].start()
        p_msgs[1, OWN, 0].start()
        for key in ((True, 1, "x"), (False, 1, "x")):
            z_msgs[key].start()
        for c in locals_:
            c.start()

    at(0.0, start_all)

    def y_arrived():
        need(y_to_opp)
        y_two_a.start()
        x_msgs["up", OPP, 1].start()
        x_msgs["down", OPP, 1].start()
        p_msgs[1, OPP, 1].start()
        need(y_to_own)
        y_two_b.start()
        p_msgs[1, OWN, 1].start()

    at(1.0, y_arrived)

    def y_two_arrived():
        need(y_two_a)
        need(y_two_b)
        x_msgs["up", OPP, 0].start()
        x_msgs["down", OPP, 0].start()
        p_msgs[1, OPP, 0].start()

    at(1.5, y_two_arrived)

    def x_arrived(hy, ly, then=()):
        def go():
            need(x_msgs["up", hy, ly])
            if (hy, ly) == (OPP, 1):
                x_msgs["far", hy, ly].start()
            p_msgs[0, hy, ly].start()
            need(x_msgs["down", hy, ly])
            if (hy, ly) in ((OPP, 0), (OWN, 1)):
                x_msgs["far", hy, ly].start()
            p_msgs[2, hy, ly].start()
            for m in then:
                x_msgs[m].start()

        return go

    at(1.03, x_arrived(OWN, 0))
    at(2.03, x_arrived(OPP, 1, (("up", OWN, 1),)))
    at(3.03, x_arrived(OPP, 0, (("down", OWN, 1), ("far", OWN, 0))))
    at(5.03, x_arrived(OWN, 1))

    def far_arrived(pairs):
        def go():
            for hy, ly in pairs:
                need(x_msgs["far", hy, ly])
                p_msgs[3, hy, ly].start()

        return go

    at(4.03, far_arrived(((OPP, 1), (OPP, 0))))
    at(6.03, far_arrived(((OWN, 0), (OWN, 1))))

    produced, pending, sent = {}, [], set()

    def flush():
        while pending:
            tile = pending.pop()
            sent.add(tile)
            for path in (0, 1):
                first[tile + (path,)].start()

    def opp_at(time, g, xs):
        def go():
            ready(g, (xs,), OPP)
            before = list(pending)
            opp_tile(g, xs)
            if before:
                flush()
            pending.append((g, xs))

        at(time, go)
        produced[g, xs] = (time + 0.12, GROUPS[g][1])

    def own_at(time, g, start, step, count):
        def go():
            ready(g, [start + i * step for i in range(count)], OWN)
            own_tiles(g, start, step, count)
            flush()

        at(time, go)

    opp_at(1.70, 0, 1)
    own_at(1.75, 0, 1, 1, 1)
    opp_at(2.10, 1, 1)
    own_at(2.20, 1, 1, 1, 1)
    for i, xs in enumerate((0, 2)):
        opp_at(3.10 + 0.15 * i, 0, xs)
        opp_at(3.16 + 0.15 * i, 1, xs)
    for i, (g, xs) in enumerate(((2, 1), (2, 0), (2, 2), (0, 3), (1, 3), (2, 3))):
        opp_at(4.10 + 0.1 * i, g, xs)
    own_at(4.72, 2, 1, 1, 1)
    own_at(5.12, 0, 0, 2, 2)
    own_at(5.30, 1, 0, 2, 2)
    own_at(5.50, 2, 0, 2, 2)
    for xs in range(4):
        opp_at(6.10 + 0.1 * xs, 3, xs)
    own_at(6.51, 0, 3, 1, 1)
    own_at(6.56, 1, 3, 1, 1)
    own_at(6.66, 2, 3, 1, 1)
    own_at(6.76, 3, 0, 1, 4)
    for xs in range(4):
        opp_at(7.10 + 0.05 * xs, 4, xs)
    own_at(7.31, 4, 0, 1, 4)

    def relay_at(time, tile):
        def go():
            if tile not in sent:
                flush()
            for path in (0, 1):
                need(first[tile + (path,)])
                for m in second[tile + (path,)]:
                    m.start()

        at(time, go)

    for tile, time in out_times(produced).items():
        relay_at(time, tile)

    own_copies = []

    def write_own(slots):
        def go():
            for l in slots:
                c = pltpu.make_async_copy(
                    own_out.at[l], out.at[:, yh * NZ + (z + Z_OFFSET[l] + NZ) % NZ], local_sem.at[3 + l]
                )
                c.start()
                own_copies.append(c)

        return go

    at(7.05, write_own(range(7)))
    at(7.45, write_own((7,)))

    for _, _, fn in sorted(events, key=lambda e: e[:2]):
        fn()

    for group in second.values():
        for m in group:
            need(m)
    for c in own_copies:
        c.wait()
    for m in messages.copies:
        m.wait_send()
        if id(m) not in waited:
            raise ValueError("unreceived message")


def per_device(quantized_inputs, x_full):
    fd, tokens = quantized_inputs.shape
    columns = 16 * fd
    stats = pl.pallas_call(
        kernel,
        out_shape=jax.ShapeDtypeStruct((2, 16, fd, columns), BF16),
        in_specs=[pl.BlockSpec(memory_space=pl.ANY)] * 2,
        out_specs=pl.BlockSpec(memory_space=pl.ANY),
        scratch_shapes=[
            pltpu.VMEM((8, 2, fd, tokens), BF16),
            pltpu.VMEM((8, fd, tokens), BF16),
            pltpu.VMEM((4, 2, 2, 2, fd, tokens), BF16),
            pltpu.VMEM((2, 4, 8, 2, fd, 2 * fd), BF16),
            pltpu.VMEM((2, 4, 8, 2, fd, 2 * fd), BF16),
            pltpu.VMEM((8, 2, fd, columns), BF16),
            pltpu.SemaphoreType.DMA((N_SEND,)),
            pltpu.SemaphoreType.DMA((N_SEND,)),
            pltpu.SemaphoreType.DMA((11,)),
        ],
        compiler_params=pltpu.CompilerParams(collective_id=0, has_side_effects=True),
    )(quantized_inputs, x_full)
    shape = (16, 1, fd, columns)
    return stats[0].astype(F32).reshape(shape), stats[1].astype(F32).reshape(shape)


def solution(mesh):
    return jax.shard_map(
        per_device,
        mesh=mesh,
        in_specs=(P(("wide", "narrow"), None), P(("wide", "narrow"), None)),
        out_specs=(P(None, "narrow", None, "wide"), P(None, "narrow", None, "wide")),
        check_vma=False,
    )
```

```python
import heapq

import jax
import jax.numpy as jnp
from jax import lax
from jax.experimental import pallas as pl
from jax.experimental.pallas import tpu as pltpu
from jax.sharding import PartitionSpec as P

MESH = pl.DeviceIdType.MESH
BF16 = jnp.bfloat16
F32 = jnp.float32

NZ, NX = 8, 4
Z_OFFSET = (0, -1, 1, -2, 2, -3, 3, 4)
Q_AT = (0, 2, 3, 6, 7, 10, 11, 14)
D_AT = (1, 4, 5, 8, 9, 12, 13, 15)
OPP, OWN = 0, 1
BLOCK = 0.0417


def out_times(produced):
    queue, free, landed, n = [], [0.0, 0.0], {}, 0
    for tile, at in produced.items():
        heapq.heappush(queue, (at, n, 0, tile))
        n += 1
    while queue:
        at, _, hop, tile = heapq.heappop(queue)
        link = tile[0] if hop == 0 else 1 - tile[0]
        free[link] = max(free[link], at) + BLOCK * (tile[3] if tile[4] is None else tile[3] / 2)
        if hop == 0:
            landed[tile] = free[link] + 0.15
            heapq.heappush(queue, (landed[tile], n, 1, tile))
            n += 1
    return landed


N_RING = 16 + 12 + 4 + 16
N_OUT = 58
Z_SEND, X_SEND, Y_SEND, P_SEND, SHIP_SEND, RELAY_SEND = range(6)


def gather_kernel(
    q_in, x_in, out, left, xs_left, right, ship, relay, send_sem, ring_sem, ship_sem, out_sem, local_sem
):
    fd, tokens = q_in.shape
    half = fd // 2
    scale = 1.0 / tokens
    wide, narrow = lax.axis_index("wide"), lax.axis_index("narrow")
    yh, z = wide // NZ, wide % NZ
    yl, x, core = narrow // (2 * NX), (narrow // 2) % NX, narrow % 2

    def device(yh_, z_, yl_, x_, core_):
        return (yh_ * NZ + z_, (yl_ * NX + x_) * 2 + core_)

    z_up, z_down = (device(yh, (z + d) % NZ, yl, x, core) for d in (1, NZ - 1))
    x_up, x_down = (device(yh, z, yl, (x + d) % NX, core) for d in (1, NX - 1))
    partner = device(yh, z, yl, x, 1 - core)
    y_opp = device(1 - yh, z, 1 - yl, x, core)
    y_own = device(yh, z, 1 - yl, x, core)

    barrier = pltpu.get_barrier_semaphore()
    neighbours = (z_up, z_down, x_up, x_down, partner, y_opp, y_own)
    for d in neighbours:
        pl.semaphore_signal(barrier, inc=1, device_id=d, device_id_type=MESH)
    pl.semaphore_wait(barrier, len(neighbours))

    ring_count = [0]
    waited = set()

    def copy(src, dst, sender, receive, to):
        return pltpu.make_async_remote_copy(
            src_ref=src,
            dst_ref=dst,
            send_sem=send_sem.at[sender],
            recv_sem=receive,
            device_id=to,
            device_id_type=MESH,
        )

    def make(src, dst, sender, to):
        ring_count[0] += 1
        return copy(src, dst, sender, ring_sem.at[ring_count[0] - 1], to)

    def need(m):
        if id(m) not in waited:
            waited.add(id(m))
            m.wait_recv()

    locals_ = [
        pltpu.make_async_copy(q_in, left.at[0], local_sem.at[0]),
        pltpu.make_async_copy(x_in, xs_left.at[0], local_sem.at[1]),
        pltpu.make_async_copy(q_in, right.at[1, OWN, 0, core], local_sem.at[2]),
    ]

    lo, hi = pl.ds(0, half), pl.ds(half, half)

    z_msgs = {}
    for up in (True, False):
        to = z_up if up else z_down
        for k in (1, 2, 3):
            src, dst = (2 * (k - 1) - 1 if up else 2 * (k - 1)), (2 * k - 1 if up else 2 * k)
            q_src = q_in if k == 1 else left.at[Q_AT[src]]
            x_src = x_in if k == 1 else xs_left.at[src]
            z_msgs[up, k, "q"] = make(q_src, left.at[Q_AT[dst]], Z_SEND, to)
            z_msgs[up, k, "x"] = make(x_src, xs_left.at[dst], Z_SEND, to)
        for h, rows in enumerate((lo, hi)):
            if up:
                z_msgs[up, 4, "q", h] = make(left.at[Q_AT[5], rows], left.at[Q_AT[7], rows], Z_SEND, to)
            else:
                z_msgs[up, 4, "x", h] = make(xs_left.at[6, rows], xs_left.at[7, rows], Z_SEND, to)

    y_to_opp = make(q_in, right.at[1, OPP, 1, core], Y_SEND, y_opp)
    y_to_own = make(q_in, right.at[1, OWN, 1, core], Y_SEND, y_own)
    y_two_a = make(right.at[1, OPP, 1, core, lo], right.at[1, OPP, 0, core, lo], Y_SEND, y_own)
    y_two_b = make(right.at[1, OWN, 1, core, hi], right.at[1, OPP, 0, core, hi], Y_SEND, y_opp)

    x_msgs = {}
    for hy in (OPP, OWN):
        for ly in (0, 1):
            src = q_in if (hy, ly) == (OWN, 0) else right.at[1, hy, ly, core]
            x_msgs["up", hy, ly] = make(src, right.at[0, hy, ly, core], X_SEND, x_up)
            x_msgs["down", hy, ly] = make(src, right.at[2, hy, ly, core], X_SEND, x_down)
    for hy, ly in ((OPP, 1), (OWN, 0)):
        x_msgs["far", hy, ly] = make(right.at[0, hy, ly, core], right.at[3, hy, ly, core], X_SEND, x_up)
    for hy, ly in ((OPP, 0), (OWN, 1)):
        x_msgs["far", hy, ly] = make(right.at[2, hy, ly, core], right.at[3, hy, ly, core], X_SEND, x_down)

    p_msgs = {}
    for xs in range(4):
        for hy in (OPP, OWN):
            for ly in (0, 1):
                src = q_in if (xs, hy, ly) == (1, OWN, 0) else right.at[xs, hy, ly, core]
                p_msgs[xs, hy, ly] = make(src, right.at[xs, hy, ly, core], P_SEND, partner)
    assert ring_count[0] == N_RING, ring_count[0]

    x_way = {0: "up", 2: "down", 3: "far"}

    def right_messages(xs, hy, ly):
        got = [p_msgs[xs, hy, ly]]
        if xs != 1:
            return [x_msgs[x_way[xs], hy, ly]] + got
        if ly == 0:
            return ([y_two_a, y_two_b] if hy == OPP else []) + got
        return [y_to_opp if hy == OPP else y_to_own] + got

    def block(ref, tile):
        path, xs, r0, n, h = tile
        if h is None:
            return ref.at[path, xs, pl.ds(r0, n)]
        return ref.at[path, xs, pl.ds(r0, n), pl.ds(h * half, half)]

    first, second = {}, {}

    def plan(tile):
        to = (y_opp, y_own)
        first[tile] = copy(
            block(ship, tile), block(relay, tile), SHIP_SEND, ship_sem.at[len(first)], to[tile[0]]
        )
        second[tile] = copy(
            block(relay, tile), block(out.at[1], tile), RELAY_SEND, out_sem.at[0], to[1 - tile[0]]
        )

    have = set()

    def once(key, fn):
        if key not in have:
            have.add(key)
            fn()

    def subtract(slot, rows):
        left[D_AT[slot], rows] = (xs_left[slot, rows].astype(F32) - left[Q_AT[slot], rows].astype(F32)).astype(
            BF16
        )

    def left_ready(r0, n, h):
        for r in range(r0, r0 + n):
            if r >= 14:
                for i in (0, 1) if h is None else (h,):
                    need(z_msgs[True, 4, "q", i])
                    need(z_msgs[False, 4, "x", i])
                    once(("d", 7, i), lambda i=i: subtract(7, pl.ds(i * half, half)))
            elif r == 0:
                once("q", locals_[0].wait)
            elif r in Q_AT:
                slot = Q_AT.index(r)
                need(z_msgs[slot % 2 == 1, (slot + 1) // 2, "q"])
            else:
                slot = D_AT.index(r)
                if slot == 0:
                    once("q", locals_[0].wait)
                    once("x", locals_[1].wait)
                else:
                    need(z_msgs[slot % 2 == 1, (slot + 1) // 2, "q"])
                    need(z_msgs[slot % 2 == 1, (slot + 1) // 2, "x"])
                once(("d", slot), lambda slot=slot: subtract(slot, pl.ds(0, fd)))

    def right_ready(xs, hy, lys):
        for ly in lys:
            if (xs, hy, ly) == (1, OWN, 0):
                once("r", locals_[2].wait)
            for m in right_messages(xs, hy, ly):
                need(m)

    def product(xs, hy, lys, r0, n, h):
        if h is None:
            a = left[r0 : r0 + n].reshape(n * fd, tokens)
        else:
            a = left[r0 : r0 + n, h * half : (h + 1) * half].reshape(n * half, tokens)
        b = right[xs, hy, lys[0] : lys[-1] + 1].reshape(len(lys) * 2 * fd, tokens)
        p = lax.dot_general(a, b, (((1,), (1,)), ((), ())), preferred_element_type=F32) * scale
        return p.astype(BF16).reshape(n, fd if h is None else half, len(lys) * 2 * fd)

    def own_tiles(r0, n, start, step, count):
        def one(i, _):
            xs = start + i * step
            p = product(xs, OWN, (0, 1), r0, n, None)
            for ly in (0, 1):
                out[0, ly, xs, r0 : r0 + n] = p[..., ly * 2 * fd : (ly + 1) * 2 * fd]
            return 0

        if count == 1:
            one(0, 0)
        else:
            lax.fori_loop(0, count, one, 0)

    events = []

    def at(time, fn):
        events.append((time, len(events), fn))

    def forward_z(what, k):
        def go():
            for up in (True, False):
                need(z_msgs[up, k, what])
                if k < 3:
                    z_msgs[up, k + 1, what].start()
                elif up == (what == "q"):
                    z_msgs[up, 4, what, 0].start()
                    z_msgs[up, 4, what, 1].start()

        return go

    for k in (1, 2, 3):
        at(2 * k - 1 + 0.05, forward_z("q", k))
        at(2 * k + 0.05, forward_z("x", k))

    def start_all():
        for key in ((True, 1, "q"), (False, 1, "q")):
            z_msgs[key].start()
        y_to_opp.start()
        y_to_own.start()
        x_msgs["up", OWN, 0].start()
        x_msgs["down", OWN, 0].start()
        p_msgs[1, OWN, 0].start()
        for key in ((True, 1, "x"), (False, 1, "x")):
            z_msgs[key].start()
        for c in locals_:
            c.start()

    at(0.0, start_all)

    def y_arrived():
        need(y_to_opp)
        y_two_a.start()
        x_msgs["up", OPP, 1].start()
        x_msgs["down", OPP, 1].start()
        p_msgs[1, OPP, 1].start()
        need(y_to_own)
        y_two_b.start()
        p_msgs[1, OWN, 1].start()

    at(1.04, y_arrived)

    def y_two_arrived():
        need(y_two_a)
        need(y_two_b)
        x_msgs["up", OPP, 0].start()
        x_msgs["down", OPP, 0].start()
        p_msgs[1, OPP, 0].start()

    at(1.6, y_two_arrived)

    def x_arrived(hy, ly, then=()):
        def go():
            need(x_msgs["up", hy, ly])
            if (hy, ly) == (OPP, 1):
                x_msgs["far", hy, ly].start()
            p_msgs[0, hy, ly].start()
            need(x_msgs["down", hy, ly])
            if (hy, ly) in ((OPP, 0), (OWN, 1)):
                x_msgs["far", hy, ly].start()
            p_msgs[2, hy, ly].start()
            for m in then:
                x_msgs[m].start()

        return go

    at(1.06, x_arrived(OWN, 0))
    at(2.15, x_arrived(OPP, 1, (("up", OWN, 1),)))
    at(3.2, x_arrived(OPP, 0, (("down", OWN, 1), ("far", OWN, 0))))
    at(5.3, x_arrived(OWN, 1))

    def far_arrived(pairs):
        def go():
            for hy, ly in pairs:
                need(x_msgs["far", hy, ly])
                p_msgs[3, hy, ly].start()

        return go

    at(4.25, far_arrived(((OPP, 1), (OPP, 0))))
    at(6.35, far_arrived(((OWN, 0), (OWN, 1))))

    produced, pending, sent = {}, [], set()

    def flush():
        while pending:
            tile = pending.pop(0)
            sent.add(tile)
            first[tile].start()

    def opp_at(time, r0, n, xs, lys=(0, 1), h=None):
        tiles = [(ly, xs, r0, n, h) for ly in lys]

        def go():
            left_ready(r0, n, h)
            right_ready(xs, OPP, lys)
            before = list(pending)
            p = product(xs, OPP, lys, r0, n, h)
            for i, tile in enumerate(tiles):
                value = p[..., i * 2 * fd : (i + 1) * 2 * fd]
                if h is None:
                    ship[tile[0], xs, r0 : r0 + n] = value
                else:
                    ship[tile[0], xs, r0 : r0 + n, h * half : (h + 1) * half] = value
            if before:
                flush()
            pending.extend(tiles)

        at(time, go)
        for tile in tiles:
            plan(tile)
            produced[tile] = time + 0.1

    def own_at(time, r0, n, start, step, count):
        def go():
            left_ready(r0, n, None)
            for i in range(count):
                right_ready(start + i * step, OWN, (0, 1))
            own_tiles(r0, n, start, step, count)
            flush()

        at(time, go)

    opp_at(1.75, 0, 2, 1)
    own_at(1.76, 0, 2, 1, 1, 1)
    opp_at(2.10, 2, 4, 1)
    for i, xs in enumerate((0, 2)):
        opp_at(2.32 + 0.08 * i, 0, 6, xs, (1,))
    own_at(2.50, 2, 4, 1, 1, 1)
    opp_at(3.10, 6, 2, 1)
    for i, xs in enumerate((0, 2)):
        opp_at(3.36 + 0.13 * i, 0, 6, xs, (0,))
        opp_at(3.44 + 0.13 * i, 6, 2, xs)
    for i, xs in enumerate((1, 0, 2)):
        opp_at(4.10 + 0.05 * i, 8, 2, xs)
    opp_at(4.42, 0, 4, 3)
    opp_at(4.49, 4, 4, 3)
    opp_at(4.56, 8, 2, 3)
    own_at(4.70, 6, 4, 1, 1, 1)
    for i, xs in enumerate((1, 0, 2, 3)):
        opp_at(5.10 + 0.05 * i, 10, 2, xs)
    own_at(5.50, 0, 4, 0, 2, 2)
    own_at(5.66, 4, 4, 0, 2, 2)
    own_at(5.80, 8, 2, 0, 2, 2)
    for i, xs in enumerate((1, 0, 2, 3)):
        opp_at(6.10 + 0.05 * i, 12, 2, xs)
    own_at(6.31, 10, 4, 0, 1, 3)
    for h in (0, 1):
        for i, xs in enumerate((1, 0, 2, 3)):
            opp_at(6.60 + 0.5 * h + 0.05 * i, 14, 2, xs, (0, 1), h)
    own_at(7.31, 14, 2, 0, 1, 3)
    own_at(7.42, 0, 4, 3, 1, 1)
    own_at(7.49, 4, 4, 3, 1, 1)
    own_at(7.56, 8, 4, 3, 1, 1)
    own_at(7.63, 12, 4, 3, 1, 1)
    assert len(first) == N_OUT, len(first)

    def relay_at(time, tile):
        def go():
            if tile not in sent:
                flush()
            need(first[tile])
            second[tile].start()

        at(time, go)

    for tile, time in out_times(produced).items():
        relay_at(time, tile)

    for _, _, fn in sorted(events, key=lambda e: e[:2]):
        fn()

    def finish(ref, sender):
        copy(ref, ref, sender, out_sem.at[0], z_up).wait_send()

    copy(out.at[1], out.at[1], RELAY_SEND, out_sem.at[0], z_up).wait_recv()
    finish(left.at[pl.ds(0, 14)], Z_SEND)
    finish(left.at[pl.ds(0, 12)], X_SEND)
    finish(left.at[pl.ds(0, 3)], Y_SEND)
    finish(left.at[pl.ds(0, 16)], P_SEND)
    finish(ship, SHIP_SEND)
    finish(relay, RELAY_SEND)


def widen_kernel(stats, gram, cross, stage, sem):
    fd = stats.shape[4]
    wide, narrow = lax.axis_index("wide"), lax.axis_index("narrow")
    yh, z = wide // NZ, wide % NZ
    yl, x = narrow // (2 * NX), (narrow // 2) % NX
    copies = []
    for src in (0, 1):
        src_yh = yh if src == 0 else 1 - yh
        for slot in range(NZ):
            row = src_yh * NZ + (z + Z_OFFSET[slot] + NZ) % NZ
            for what, (at, dst) in enumerate(((Q_AT, gram), (D_AT, cross))):
                for ly in (0, 1):
                    col_yl = yl if ly == 0 else 1 - yl
                    for xs in range(4):
                        col = col_yl * (2 * NX * fd) + ((x + xs + NX - 1) % NX) * (2 * fd)
                        stage[what, src * NZ + slot, :, pl.ds(pl.multiple_of(col, 2 * fd), 2 * fd)] = stats[
                            src, ly, xs, at[slot]
                        ].astype(F32)
                i = what * 2 * NZ + src * NZ + slot
                c = pltpu.make_async_copy(stage.at[what, src * NZ + slot], dst.at[row, 0], sem.at[i])
                c.start()
                copies.append(c)
    for c in copies:
        c.wait()


def per_device(quantized_inputs, x_full):
    fd, tokens = quantized_inputs.shape
    columns = 16 * fd
    half_out = (2, 4, 16, fd, 2 * fd)
    stats = pl.pallas_call(
        gather_kernel,
        out_shape=pltpu.VMEM((2,) + half_out, BF16),
        in_specs=[pl.BlockSpec(memory_space=pltpu.HBM)] * 2,
        out_specs=pl.BlockSpec(memory_space=pltpu.VMEM),
        scratch_shapes=[
            pltpu.VMEM((16, fd, tokens), BF16),
            pltpu.VMEM((8, fd, tokens), BF16),
            pltpu.VMEM((4, 2, 2, 2, fd, tokens), BF16),
            pltpu.VMEM(half_out, BF16),
            pltpu.VMEM(half_out, BF16),
            pltpu.SemaphoreType.DMA((6,)),
            pltpu.SemaphoreType.DMA((N_RING,)),
            pltpu.SemaphoreType.DMA((N_OUT,)),
            pltpu.SemaphoreType.DMA((1,)),
            pltpu.SemaphoreType.DMA((3,)),
        ],
        compiler_params=pltpu.CompilerParams(
            collective_id=0, has_side_effects=True, vmem_limit_bytes=(59 * 1024 + 640) * 1024
        ),
    )(quantized_inputs, x_full)
    shape = (16, 1, fd, columns)
    return tuple(
        pl.pallas_call(
            widen_kernel,
            out_shape=[jax.ShapeDtypeStruct(shape, F32)] * 2,
            in_specs=[pl.BlockSpec(memory_space=pltpu.VMEM)],
            out_specs=[pl.BlockSpec(memory_space=pl.ANY)] * 2,
            scratch_shapes=[
                pltpu.VMEM((2, 16, fd, columns), F32),
                pltpu.SemaphoreType.DMA((32,)),
            ],
            compiler_params=pltpu.CompilerParams(vmem_limit_bytes=24 * 2**20),
        )(stats)
    )


def solution(mesh):
    return jax.shard_map(
        per_device,
        mesh=mesh,
        in_specs=(P(("wide", "narrow"), None), P(("wide", "narrow"), None)),
        out_specs=(P(None, "narrow", None, "wide"), P(None, "narrow", None, "wide")),
        check_vma=False,
    )
```

```python
import jax
import jax.numpy as jnp
from jax import lax
from jax.experimental import pallas as pl
from jax.experimental.pallas import tpu as pltpu
from jax.sharding import PartitionSpec as P

MESH = pl.DeviceIdType.MESH
BF16 = jnp.bfloat16
F32 = jnp.float32

NZ, NX = 8, 4
Z_OFFSET = (0, -1, 1, -2, 2, -3, 3, 4)
Q_AT = (0, 2, 3, 6, 7, 10, 11, 14)
D_AT = (1, 4, 5, 8, 9, 12, 13, 15)
OPP, OWN = 0, 1


N_RING = 16 + 12 + 4 + 16
Z_SEND, X_SEND, Y_SEND, P_SEND, SHIP_SEND = range(5)


def gather_kernel(
    q_in, x_in, out, left, xs_left, right, ship, send_sem, ring_sem, out_sem, local_sem
):
    fd, tokens = q_in.shape
    half = fd // 2
    scale = 1.0 / tokens
    wide, narrow = lax.axis_index("wide"), lax.axis_index("narrow")
    yh, z = wide // NZ, wide % NZ
    yl, x, core = narrow // (2 * NX), (narrow // 2) % NX, narrow % 2

    def device(yh_, z_, yl_, x_, core_):
        return (yh_ * NZ + z_, (yl_ * NX + x_) * 2 + core_)

    z_up, z_down = (device(yh, (z + d) % NZ, yl, x, core) for d in (1, NZ - 1))
    x_up, x_down = (device(yh, z, yl, (x + d) % NX, core) for d in (1, NX - 1))
    partner = device(yh, z, yl, x, 1 - core)
    y_opp = device(1 - yh, z, 1 - yl, x, core)
    y_own = device(yh, z, 1 - yl, x, core)

    barrier = pltpu.get_barrier_semaphore()
    y_far = device(1 - yh, z, yl, x, core)
    neighbours = (z_up, z_down, x_up, x_down, partner, y_opp, y_own, y_far)
    for d in neighbours:
        pl.semaphore_signal(barrier, inc=1, device_id=d, device_id_type=MESH)
    pl.semaphore_wait(barrier, len(neighbours))

    ring_count = [0]
    waited = set()

    def copy(src, dst, sender, receive, to):
        return pltpu.make_async_remote_copy(
            src_ref=src,
            dst_ref=dst,
            send_sem=send_sem.at[sender],
            recv_sem=receive,
            device_id=to,
            device_id_type=MESH,
        )

    def make(src, dst, sender, to):
        ring_count[0] += 1
        return copy(src, dst, sender, ring_sem.at[ring_count[0] - 1], to)

    def need(m):
        if id(m) not in waited:
            waited.add(id(m))
            m.wait_recv()

    locals_ = [
        pltpu.make_async_copy(q_in, left.at[0], local_sem.at[0]),
        pltpu.make_async_copy(x_in, xs_left.at[0], local_sem.at[1]),
        pltpu.make_async_copy(q_in, right.at[1, OWN, 0, core], local_sem.at[2]),
    ]

    lo, hi = pl.ds(0, half), pl.ds(half, half)

    z_msgs = {}
    for up in (True, False):
        to = z_up if up else z_down
        for k in (1, 2, 3):
            src, dst = (2 * (k - 1) - 1 if up else 2 * (k - 1)), (2 * k - 1 if up else 2 * k)
            q_src = q_in if k == 1 else left.at[Q_AT[src]]
            x_src = x_in if k == 1 else xs_left.at[src]
            z_msgs[up, k, "q"] = make(q_src, left.at[Q_AT[dst]], Z_SEND, to)
            z_msgs[up, k, "x"] = make(x_src, xs_left.at[dst], Z_SEND, to)
        for h, rows in enumerate((lo, hi)):
            if up:
                z_msgs[up, 4, "q", h] = make(left.at[Q_AT[5], rows], left.at[Q_AT[7], rows], Z_SEND, to)
            else:
                z_msgs[up, 4, "x", h] = make(xs_left.at[6, rows], xs_left.at[7, rows], Z_SEND, to)

    y_to_opp = make(q_in, right.at[1, OPP, 1, core], Y_SEND, y_opp)
    y_to_own = make(q_in, right.at[1, OWN, 1, core], Y_SEND, y_own)
    y_two_a = make(right.at[1, OPP, 1, core, lo], right.at[1, OPP, 0, core, lo], Y_SEND, y_own)
    y_two_b = make(right.at[1, OWN, 1, core, hi], right.at[1, OPP, 0, core, hi], Y_SEND, y_opp)

    x_msgs = {}
    for hy in (OPP, OWN):
        for ly in (0, 1):
            src = q_in if (hy, ly) == (OWN, 0) else right.at[1, hy, ly, core]
            x_msgs["up", hy, ly] = make(src, right.at[0, hy, ly, core], X_SEND, x_up)
            x_msgs["down", hy, ly] = make(src, right.at[2, hy, ly, core], X_SEND, x_down)
    for hy, ly in ((OPP, 1), (OWN, 0)):
        x_msgs["far", hy, ly] = make(right.at[0, hy, ly, core], right.at[3, hy, ly, core], X_SEND, x_up)
    for hy, ly in ((OPP, 0), (OWN, 1)):
        x_msgs["far", hy, ly] = make(right.at[2, hy, ly, core], right.at[3, hy, ly, core], X_SEND, x_down)

    p_msgs = {}
    for xs in range(4):
        for hy in (OPP, OWN):
            for ly in (0, 1):
                src = q_in if (xs, hy, ly) == (1, OWN, 0) else right.at[xs, hy, ly, core]
                p_msgs[xs, hy, ly] = make(src, right.at[xs, hy, ly, core], P_SEND, partner)
    assert ring_count[0] == N_RING, ring_count[0]

    x_way = {0: "up", 2: "down", 3: "far"}

    def right_messages(xs, hy, ly):
        got = [p_msgs[xs, hy, ly]]
        if xs != 1:
            return [x_msgs[x_way[xs], hy, ly]] + got
        if ly == 0:
            return ([y_two_a, y_two_b] if hy == OPP else []) + got
        return [y_to_opp if hy == OPP else y_to_own] + got

    def block(ref, tile):
        ly, xs, r0, n, h = tile
        if h is None:
            return ref.at[ly, xs, pl.ds(r0, n)]
        return ref.at[ly, xs, pl.ds(r0, n), pl.ds(h * half, half)]

    def ship_out(tile):
        copy(block(ship, tile), block(out.at[1], tile), SHIP_SEND, out_sem.at[0], y_far).start()

    have = set()

    def once(key, fn):
        if key not in have:
            have.add(key)
            fn()

    def subtract(slot, rows):
        left[D_AT[slot], rows] = (xs_left[slot, rows].astype(F32) - left[Q_AT[slot], rows].astype(F32)).astype(
            BF16
        )

    def left_ready(r0, n, h):
        for r in range(r0, r0 + n):
            if r >= 14:
                for i in (0, 1) if h is None else (h,):
                    need(z_msgs[True, 4, "q", i])
                    need(z_msgs[False, 4, "x", i])
                    once(("d", 7, i), lambda i=i: subtract(7, pl.ds(i * half, half)))
            elif r == 0:
                once("q", locals_[0].wait)
            elif r in Q_AT:
                slot = Q_AT.index(r)
                need(z_msgs[slot % 2 == 1, (slot + 1) // 2, "q"])
            else:
                slot = D_AT.index(r)
                if slot == 0:
                    once("q", locals_[0].wait)
                    once("x", locals_[1].wait)
                else:
                    need(z_msgs[slot % 2 == 1, (slot + 1) // 2, "q"])
                    need(z_msgs[slot % 2 == 1, (slot + 1) // 2, "x"])
                once(("d", slot), lambda slot=slot: subtract(slot, pl.ds(0, fd)))

    def right_ready(xs, hy, lys):
        for ly in lys:
            if (xs, hy, ly) == (1, OWN, 0):
                once("r", locals_[2].wait)
            for m in right_messages(xs, hy, ly):
                need(m)

    def product(xs, hy, lys, r0, n, h):
        if h is None:
            a = left[r0 : r0 + n].reshape(n * fd, tokens)
        else:
            a = left[r0 : r0 + n, h * half : (h + 1) * half].reshape(n * half, tokens)
        b = right[xs, hy, lys[0] : lys[-1] + 1].reshape(len(lys) * 2 * fd, tokens)
        p = lax.dot_general(a, b, (((1,), (1,)), ((), ())), preferred_element_type=F32) * scale
        return p.astype(BF16).reshape(n, fd if h is None else half, len(lys) * 2 * fd)

    def own_tiles(r0, n, start, step, count):
        def one(i, _):
            xs = start + i * step
            p = product(xs, OWN, (0, 1), r0, n, None)
            for ly in (0, 1):
                out[0, ly, xs, r0 : r0 + n] = p[..., ly * 2 * fd : (ly + 1) * 2 * fd]
            return 0

        if count == 1:
            one(0, 0)
        else:
            lax.fori_loop(0, count, one, 0)

    events = []

    def at(time, fn):
        events.append((time, len(events), fn))

    def forward_z(what, k):
        def go():
            for up in (True, False):
                need(z_msgs[up, k, what])
                if k < 3:
                    z_msgs[up, k + 1, what].start()
                elif up == (what == "q"):
                    z_msgs[up, 4, what, 0].start()
                    z_msgs[up, 4, what, 1].start()

        return go

    for k in (1, 2, 3):
        at(2 * k - 1 + 0.05, forward_z("q", k))
        at(2 * k + 0.05, forward_z("x", k))

    def start_all():
        for key in ((True, 1, "q"), (False, 1, "q")):
            z_msgs[key].start()
        y_to_opp.start()
        y_to_own.start()
        x_msgs["up", OWN, 0].start()
        x_msgs["down", OWN, 0].start()
        p_msgs[1, OWN, 0].start()
        for key in ((True, 1, "x"), (False, 1, "x")):
            z_msgs[key].start()
        for c in locals_:
            c.start()

    at(0.0, start_all)

    def y_arrived():
        need(y_to_opp)
        y_two_a.start()
        x_msgs["up", OPP, 1].start()
        x_msgs["down", OPP, 1].start()
        p_msgs[1, OPP, 1].start()
        need(y_to_own)
        y_two_b.start()
        p_msgs[1, OWN, 1].start()

    at(1.04, y_arrived)

    def y_two_arrived():
        need(y_two_a)
        need(y_two_b)
        x_msgs["up", OPP, 0].start()
        x_msgs["down", OPP, 0].start()
        p_msgs[1, OPP, 0].start()

    at(1.6, y_two_arrived)

    def x_arrived(hy, ly, then=()):
        def go():
            need(x_msgs["up", hy, ly])
            if (hy, ly) == (OPP, 1):
                x_msgs["far", hy, ly].start()
            p_msgs[0, hy, ly].start()
            need(x_msgs["down", hy, ly])
            if (hy, ly) in ((OPP, 0), (OWN, 1)):
                x_msgs["far", hy, ly].start()
            p_msgs[2, hy, ly].start()
            for m in then:
                x_msgs[m].start()

        return go

    at(1.06, x_arrived(OWN, 0))
    at(2.15, x_arrived(OPP, 1, (("up", OWN, 1),)))
    at(3.2, x_arrived(OPP, 0, (("down", OWN, 1), ("far", OWN, 0))))
    at(5.3, x_arrived(OWN, 1))

    def far_arrived(pairs):
        def go():
            for hy, ly in pairs:
                need(x_msgs["far", hy, ly])
                p_msgs[3, hy, ly].start()

        return go

    at(4.25, far_arrived(((OPP, 1), (OPP, 0))))
    at(6.35, far_arrived(((OWN, 0), (OWN, 1))))

    pending = []

    def flush():
        while pending:
            ship_out(pending.pop(0))

    def opp_at(time, r0, n, xs, lys=(0, 1), h=None):
        tiles = [(ly, xs, r0, n, h) for ly in lys]

        def go():
            left_ready(r0, n, h)
            right_ready(xs, OPP, lys)
            before = list(pending)
            p = product(xs, OPP, lys, r0, n, h)
            for i, tile in enumerate(tiles):
                value = p[..., i * 2 * fd : (i + 1) * 2 * fd]
                if h is None:
                    ship[tile[0], xs, r0 : r0 + n] = value
                else:
                    ship[tile[0], xs, r0 : r0 + n, h * half : (h + 1) * half] = value
            if before:
                flush()
            pending.extend(tiles)

        at(time, go)

    def own_at(time, r0, n, start, step, count):
        def go():
            left_ready(r0, n, None)
            for i in range(count):
                right_ready(start + i * step, OWN, (0, 1))
            own_tiles(r0, n, start, step, count)
            flush()

        at(time, go)

    opp_at(1.75, 0, 2, 1)
    own_at(1.76, 0, 2, 1, 1, 1)
    opp_at(2.10, 2, 4, 1)
    for i, xs in enumerate((0, 2)):
        opp_at(2.32 + 0.08 * i, 0, 6, xs, (1,))
    own_at(2.50, 2, 4, 1, 1, 1)
    opp_at(3.10, 6, 2, 1)
    for i, xs in enumerate((0, 2)):
        opp_at(3.36 + 0.13 * i, 0, 6, xs, (0,))
        opp_at(3.44 + 0.13 * i, 6, 2, xs)
    for i, xs in enumerate((1, 0, 2)):
        opp_at(4.10 + 0.05 * i, 8, 2, xs)
    opp_at(4.42, 0, 4, 3)
    opp_at(4.49, 4, 4, 3)
    opp_at(4.56, 8, 2, 3)
    own_at(4.70, 6, 4, 1, 1, 1)
    for i, xs in enumerate((1, 0, 2, 3)):
        opp_at(5.10 + 0.05 * i, 10, 2, xs)
    own_at(5.50, 0, 4, 0, 2, 2)
    own_at(5.66, 4, 4, 0, 2, 2)
    own_at(5.80, 8, 2, 0, 2, 2)
    for i, xs in enumerate((1, 0, 2, 3)):
        opp_at(6.10 + 0.05 * i, 12, 2, xs)
    own_at(6.31, 10, 4, 0, 1, 3)
    for h in (0, 1):
        for i, xs in enumerate((1, 0, 2, 3)):
            opp_at(6.60 + 0.5 * h + 0.05 * i, 14, 2, xs, (0, 1), h)
    own_at(6.52, 0, 4, 3, 1, 1)
    own_at(6.55, 4, 4, 3, 1, 1)
    own_at(6.85, 8, 4, 3, 1, 1)
    own_at(6.90, 12, 2, 3, 1, 1)
    own_at(7.31, 14, 2, 0, 1, 4)

    for _, _, fn in sorted(events, key=lambda e: e[:2]):
        fn()

    def finish(ref, sender):
        copy(ref, ref, sender, out_sem.at[0], z_up).wait_send()

    copy(out.at[1], out.at[1], SHIP_SEND, out_sem.at[0], z_up).wait_recv()
    finish(left.at[pl.ds(0, 14)], Z_SEND)
    finish(left.at[pl.ds(0, 12)], X_SEND)
    finish(left.at[pl.ds(0, 3)], Y_SEND)
    finish(left.at[pl.ds(0, 16)], P_SEND)
    finish(ship, SHIP_SEND)


def widen_kernel(stats, gram, cross, stage, sem):
    fd = stats.shape[4]
    wide, narrow = lax.axis_index("wide"), lax.axis_index("narrow")
    yh, z = wide // NZ, wide % NZ
    yl, x = narrow // (2 * NX), (narrow // 2) % NX
    copies = []
    for src in (0, 1):
        src_yh = yh if src == 0 else 1 - yh
        for slot in range(NZ):
            row = src_yh * NZ + (z + Z_OFFSET[slot] + NZ) % NZ
            for what, (at, dst) in enumerate(((Q_AT, gram), (D_AT, cross))):
                for ly in (0, 1):
                    col_yl = yl if ly == 0 else 1 - yl
                    for xs in range(4):
                        col = col_yl * (2 * NX * fd) + ((x + xs + NX - 1) % NX) * (2 * fd)
                        stage[what, src * NZ + slot, :, pl.ds(pl.multiple_of(col, 2 * fd), 2 * fd)] = stats[
                            src, ly, xs, at[slot]
                        ].astype(F32)
                i = what * 2 * NZ + src * NZ + slot
                c = pltpu.make_async_copy(stage.at[what, src * NZ + slot], dst.at[row, 0], sem.at[i])
                c.start()
                copies.append(c)
    for c in copies:
        c.wait()


def per_device(quantized_inputs, x_full):
    fd, tokens = quantized_inputs.shape
    columns = 16 * fd
    half_out = (2, 4, 16, fd, 2 * fd)
    stats = pl.pallas_call(
        gather_kernel,
        out_shape=pltpu.VMEM((2,) + half_out, BF16),
        in_specs=[pl.BlockSpec(memory_space=pltpu.HBM)] * 2,
        out_specs=pl.BlockSpec(memory_space=pltpu.VMEM),
        scratch_shapes=[
            pltpu.VMEM((16, fd, tokens), BF16),
            pltpu.VMEM((8, fd, tokens), BF16),
            pltpu.VMEM((4, 2, 2, 2, fd, tokens), BF16),
            pltpu.VMEM(half_out, BF16),
            pltpu.SemaphoreType.DMA((5,)),
            pltpu.SemaphoreType.DMA((N_RING,)),
            pltpu.SemaphoreType.DMA((1,)),
            pltpu.SemaphoreType.DMA((3,)),
        ],
        compiler_params=pltpu.CompilerParams(
            collective_id=0, has_side_effects=True, vmem_limit_bytes=(59 * 1024 + 640) * 1024
        ),
    )(quantized_inputs, x_full)
    shape = (16, 1, fd, columns)
    return tuple(
        pl.pallas_call(
            widen_kernel,
            out_shape=[jax.ShapeDtypeStruct(shape, F32)] * 2,
            in_specs=[pl.BlockSpec(memory_space=pltpu.VMEM)],
            out_specs=[pl.BlockSpec(memory_space=pl.ANY)] * 2,
            scratch_shapes=[
                pltpu.VMEM((2, 16, fd, columns), F32),
                pltpu.SemaphoreType.DMA((32,)),
            ],
            compiler_params=pltpu.CompilerParams(vmem_limit_bytes=24 * 2**20),
        )(stats)
    )


def solution(mesh):
    return jax.shard_map(
        per_device,
        mesh=mesh,
        in_specs=(P(("wide", "narrow"), None), P(("wide", "narrow"), None)),
        out_specs=(P(None, "narrow", None, "wide"), P(None, "narrow", None, "wide")),
        check_vma=False,
    )
```

```python
import jax
import jax.numpy as jnp
from jax import lax
from jax.experimental import pallas as pl
from jax.experimental.pallas import tpu as pltpu
from jax.sharding import PartitionSpec as P

MESH = pl.DeviceIdType.MESH
BF16 = jnp.bfloat16
F32 = jnp.float32

NZ, NX = 8, 4
Z_OFFSET = (0, -1, 1, -2, 2, -3, 3, 4)
Q_AT = (0, 2, 3, 6, 7, 10, 11, 14)
D_AT = (1, 4, 5, 8, 9, 12, 13, 15)
OPP, OWN = 0, 1


N_RING = 16 + 6 + 20 + 16
Z_SEND, X_SEND, Y_SEND, P_SEND, SHIP_SEND = range(5)


def gather_kernel(
    q_in, x_in, out, left, xs_left, right, ship, send_sem, ring_sem, out_sem, local_sem
):
    fd, tokens = q_in.shape
    half = fd // 2
    scale = 1.0 / tokens
    wide, narrow = lax.axis_index("wide"), lax.axis_index("narrow")
    yh, z = wide // NZ, wide % NZ
    yl, x, core = narrow // (2 * NX), (narrow // 2) % NX, narrow % 2

    def device(yh_, z_, yl_, x_, core_):
        return (yh_ * NZ + z_, (yl_ * NX + x_) * 2 + core_)

    z_up, z_down = (device(yh, (z + d) % NZ, yl, x, core) for d in (1, NZ - 1))
    x_up, x_down = (device(yh, z, yl, (x + d) % NX, core) for d in (1, NX - 1))
    partner = device(yh, z, yl, x, 1 - core)
    y_opp = device(1 - yh, z, 1 - yl, x, core)
    y_own = device(yh, z, 1 - yl, x, core)

    barrier = pltpu.get_barrier_semaphore()
    y_far = device(1 - yh, z, yl, x, core)
    neighbours = (z_up, z_down, x_up, x_down, partner, y_opp, y_own, y_far)
    for d in neighbours:
        pl.semaphore_signal(barrier, inc=1, device_id=d, device_id_type=MESH)
    pl.semaphore_wait(barrier, len(neighbours))

    ring_count = [0]
    waited = set()

    def copy(src, dst, sender, receive, to):
        return pltpu.make_async_remote_copy(
            src_ref=src,
            dst_ref=dst,
            send_sem=send_sem.at[sender],
            recv_sem=receive,
            device_id=to,
            device_id_type=MESH,
        )

    def make(src, dst, sender, to):
        ring_count[0] += 1
        return copy(src, dst, sender, ring_sem.at[ring_count[0] - 1], to)

    def need(m):
        if id(m) not in waited:
            waited.add(id(m))
            m.wait_recv()

    locals_ = [
        pltpu.make_async_copy(q_in, left.at[0], local_sem.at[0]),
        pltpu.make_async_copy(x_in, xs_left.at[0], local_sem.at[1]),
        pltpu.make_async_copy(q_in, right.at[1, OWN, 0, core], local_sem.at[2]),
    ]

    lo, hi = pl.ds(0, half), pl.ds(half, half)

    z_msgs = {}
    for up in (True, False):
        to = z_up if up else z_down
        for k in (1, 2, 3):
            src, dst = (2 * (k - 1) - 1 if up else 2 * (k - 1)), (2 * k - 1 if up else 2 * k)
            q_src = q_in if k == 1 else left.at[Q_AT[src]]
            x_src = x_in if k == 1 else xs_left.at[src]
            z_msgs[up, k, "q"] = make(q_src, left.at[Q_AT[dst]], Z_SEND, to)
            z_msgs[up, k, "x"] = make(x_src, xs_left.at[dst], Z_SEND, to)
        for h, rows in enumerate((lo, hi)):
            if up:
                z_msgs[up, 4, "q", h] = make(left.at[Q_AT[5], rows], left.at[Q_AT[7], rows], Z_SEND, to)
            else:
                z_msgs[up, 4, "x", h] = make(xs_left.at[6, rows], xs_left.at[7, rows], Z_SEND, to)

    y_msgs = {}
    for to, hy in ((y_opp, OPP), (y_own, OWN)):
        for h in (lo, hi) if hy == OPP else (hi, lo):
            y_msgs[hy, h is hi] = make(q_in.at[h], right.at[1, hy, 1, core, h], Y_SEND, to)
    y_two_a = make(right.at[1, OPP, 1, core, lo], right.at[1, OPP, 0, core, lo], Y_SEND, y_own)
    y_two_b = make(right.at[1, OWN, 1, core, hi], right.at[1, OPP, 0, core, hi], Y_SEND, y_opp)

    x_msgs = {}
    for hy in (OPP, OWN):
        for ly in (0, 1):
            in_halves = (hy, ly) in ((OWN, 0), (OPP, 1))
            for way, slot, to in (("up", 0, x_up), ("down", 2, x_down)):
                x_msgs[way, hy, ly] = []
                for h in (lo, hi) if in_halves else (pl.ds(0, fd),):
                    src = q_in.at[h] if (hy, ly) == (OWN, 0) else right.at[1, hy, ly, core, h]
                    x_msgs[way, hy, ly].append(make(src, right.at[slot, hy, ly, core, h], X_SEND, to))
            x_msgs["far", hy, ly] = [
                make(right.at[slot, hy, ly, core, h], right.at[3, hy, ly, core, h], X_SEND, to)
                for slot, h, to in ((0, lo, x_up), (2, hi, x_down))
            ]

    p_msgs = {}
    for xs in range(4):
        for hy in (OPP, OWN):
            for ly in (0, 1):
                src = q_in if (xs, hy, ly) == (1, OWN, 0) else right.at[xs, hy, ly, core]
                p_msgs[xs, hy, ly] = make(src, right.at[xs, hy, ly, core], P_SEND, partner)
    assert ring_count[0] == N_RING, ring_count[0]

    x_way = {0: "up", 2: "down", 3: "far"}

    def right_messages(xs, hy, ly):
        got = [p_msgs[xs, hy, ly]]
        if xs != 1:
            return x_msgs[x_way[xs], hy, ly] + got
        if ly == 0:
            return ([y_two_a, y_two_b] if hy == OPP else []) + got
        return [y_msgs[hy, False], y_msgs[hy, True]] + got

    def block(ref, tile):
        ly, xs, r0, n, h = tile
        if h is None:
            return ref.at[ly, xs, pl.ds(r0, n)]
        return ref.at[ly, xs, pl.ds(r0, n), pl.ds(h * half, half)]

    def ship_out(tile):
        copy(block(ship, tile), block(out.at[1], tile), SHIP_SEND, out_sem.at[0], y_far).start()

    have = set()

    def once(key, fn):
        if key not in have:
            have.add(key)
            fn()

    def subtract(slot, rows):
        left[D_AT[slot], rows] = (xs_left[slot, rows].astype(F32) - left[Q_AT[slot], rows].astype(F32)).astype(
            BF16
        )

    def left_ready(r0, n, h):
        for r in range(r0, r0 + n):
            if r >= 14:
                for i in (0, 1) if h is None else (h,):
                    need(z_msgs[True, 4, "q", i])
                    need(z_msgs[False, 4, "x", i])
                    once(("d", 7, i), lambda i=i: subtract(7, pl.ds(i * half, half)))
            elif r == 0:
                once("q", locals_[0].wait)
            elif r in Q_AT:
                slot = Q_AT.index(r)
                need(z_msgs[slot % 2 == 1, (slot + 1) // 2, "q"])
            else:
                slot = D_AT.index(r)
                if slot == 0:
                    once("q", locals_[0].wait)
                    once("x", locals_[1].wait)
                else:
                    need(z_msgs[slot % 2 == 1, (slot + 1) // 2, "q"])
                    need(z_msgs[slot % 2 == 1, (slot + 1) // 2, "x"])
                once(("d", slot), lambda slot=slot: subtract(slot, pl.ds(0, fd)))

    def right_ready(xs, hy, lys):
        for ly in lys:
            if (xs, hy, ly) == (1, OWN, 0):
                once("r", locals_[2].wait)
            for m in right_messages(xs, hy, ly):
                need(m)

    def product(xs, hy, lys, r0, n, h):
        if h is None:
            a = left[r0 : r0 + n].reshape(n * fd, tokens)
        else:
            a = left[r0 : r0 + n, h * half : (h + 1) * half].reshape(n * half, tokens)
        b = right[xs, hy, lys[0] : lys[-1] + 1].reshape(len(lys) * 2 * fd, tokens)
        p = lax.dot_general(a, b, (((1,), (1,)), ((), ())), preferred_element_type=F32) * scale
        return p.astype(BF16).reshape(n, fd if h is None else half, len(lys) * 2 * fd)

    def own_tiles(r0, n, start, step, count):
        def one(i, _):
            xs = start + i * step
            p = product(xs, OWN, (0, 1), r0, n, None)
            for ly in (0, 1):
                out[0, ly, xs, r0 : r0 + n] = p[..., ly * 2 * fd : (ly + 1) * 2 * fd]
            return 0

        if count == 1:
            one(0, 0)
        else:
            lax.fori_loop(0, count, one, 0)

    events = []

    def at(time, fn):
        events.append((time, len(events), fn))

    def forward_z(what, k):
        def go():
            for up in (True, False):
                need(z_msgs[up, k, what])
                if k < 3:
                    z_msgs[up, k + 1, what].start()
                elif up == (what == "q"):
                    z_msgs[up, 4, what, 0].start()
                    z_msgs[up, 4, what, 1].start()

        return go

    for k in (1, 2, 3):
        at(2 * k - 1 + 0.05, forward_z("q", k))
        at(2 * k + 0.05, forward_z("x", k))

    def start_all():
        for key in ((True, 1, "q"), (False, 1, "q")):
            z_msgs[key].start()
        for m in y_msgs.values():
            m.start()
        x_msgs["up", OWN, 0][0].start()
        x_msgs["down", OWN, 0][0].start()
        p_msgs[1, OWN, 0].start()
        for key in ((True, 1, "x"), (False, 1, "x")):
            z_msgs[key].start()
        for c in locals_:
            c.start()

    at(0.0, start_all)

    def to_x(hy, ly, i=0):
        x_msgs["up", hy, ly][i].start()
        x_msgs["down", hy, ly][i].start()

    def y_first_half():
        need(y_msgs[OPP, False])
        y_two_a.start()
        to_x(OPP, 1, 0)
        need(y_msgs[OWN, True])
        y_two_b.start()

    at(0.55, y_first_half)

    def y_second_half():
        need(y_msgs[OPP, True])
        to_x(OPP, 1, 1)
        p_msgs[1, OPP, 1].start()
        need(y_msgs[OWN, False])
        p_msgs[1, OWN, 1].start()

    at(1.04, y_second_half)

    def y_two_arrived():
        need(y_two_a)
        need(y_two_b)
        to_x(OPP, 0)
        p_msgs[1, OPP, 0].start()

    at(1.6, y_two_arrived)

    def x_arrived(hy, ly):
        def go():
            for i, way in enumerate(("up", "down")):
                for m in x_msgs[way, hy, ly]:
                    need(m)
                x_msgs["far", hy, ly][i].start()
                p_msgs[2 * i, hy, ly].start()

        return go

    at(1.65, x_arrived(OPP, 1))
    at(2.70, x_arrived(OPP, 0))
    at(2.71, lambda: to_x(OWN, 0, 1))
    at(4.20, x_arrived(OWN, 0))
    at(5.20, x_arrived(OWN, 1))

    def far_arrived(hy, ly):
        def go():
            for m in x_msgs["far", hy, ly]:
                need(m)
            p_msgs[3, hy, ly].start()

        return go

    at(3.18, far_arrived(OPP, 1))
    at(3.19, lambda: to_x(OWN, 1))
    at(3.70, far_arrived(OPP, 0))
    at(5.70, far_arrived(OWN, 0))
    at(6.22, far_arrived(OWN, 1))

    pending = []

    def flush():
        while pending:
            ship_out(pending.pop(0))

    def opp_at(time, r0, n, xs, lys=(0, 1), h=None):
        tiles = [(ly, xs, r0, n, h) for ly in lys]

        def go():
            left_ready(r0, n, h)
            right_ready(xs, OPP, lys)
            before = list(pending)
            p = product(xs, OPP, lys, r0, n, h)
            for i, tile in enumerate(tiles):
                value = p[..., i * 2 * fd : (i + 1) * 2 * fd]
                if h is None:
                    ship[tile[0], xs, r0 : r0 + n] = value
                else:
                    ship[tile[0], xs, r0 : r0 + n, h * half : (h + 1) * half] = value
            if before:
                flush()
            pending.extend(tiles)

        at(time, go)

    def own_at(time, r0, n, start, step, count):
        def go():
            left_ready(r0, n, None)
            for i in range(count):
                right_ready(start + i * step, OWN, (0, 1))
            own_tiles(r0, n, start, step, count)
            flush()

        at(time, go)

    opp_at(1.25, 0, 4, 1, (1,))
    own_at(1.35, 0, 4, 1, 1, 1)
    opp_at(1.72, 0, 4, 1, (0,))
    for i, xs in enumerate((0, 2)):
        opp_at(1.80 + 0.08 * i, 0, 4, xs, (1,))
    opp_at(2.10, 4, 2, 1)
    for i, xs in enumerate((0, 2)):
        opp_at(2.18 + 0.08 * i, 4, 2, xs, (1,))
    for i, xs in enumerate((0, 2)):
        opp_at(2.82 + 0.10 * i, 0, 6, xs, (0,))
    for i, xs in enumerate((1, 0, 2)):
        opp_at(3.10 + 0.08 * i, 6, 2, xs)
    opp_at(3.35, 0, 8, 3, (1,))
    opp_at(3.85, 0, 8, 3, (0,))
    own_at(3.95, 4, 4, 1, 1, 1)
    for i, xs in enumerate((1, 0, 2, 3)):
        opp_at(4.10 + 0.08 * i, 8, 2, xs)
    for i, xs in enumerate((1, 0, 2, 3)):
        opp_at(5.10 + 0.08 * i, 10, 2, xs)
    own_at(5.45, 0, 4, 0, 2, 2)
    own_at(5.60, 4, 4, 0, 2, 2)
    own_at(5.76, 8, 4, 0, 1, 3)
    for i, xs in enumerate((1, 0, 2, 3)):
        opp_at(6.10 + 0.08 * i, 12, 2, xs)
    own_at(6.43, 0, 4, 3, 1, 1)
    own_at(6.51, 4, 4, 3, 1, 1)
    for i, xs in enumerate((1, 0, 2, 3)):
        opp_at(6.60 + 0.08 * i, 14, 2, xs, (0, 1), 0)
    own_at(6.95, 8, 4, 3, 1, 1)
    for i, xs in enumerate((1, 0, 2, 3)):
        opp_at(7.10 + 0.08 * i, 14, 2, xs, (0, 1), 1)
    own_at(7.45, 12, 4, 0, 1, 4)

    for _, _, fn in sorted(events, key=lambda e: e[:2]):
        fn()

    def finish(ref, sender):
        copy(ref, ref, sender, out_sem.at[0], z_up).wait_send()

    copy(out.at[1], out.at[1], SHIP_SEND, out_sem.at[0], z_up).wait_recv()
    finish(left.at[pl.ds(0, 14)], Z_SEND)
    finish(left.at[pl.ds(0, 12)], X_SEND)
    finish(left.at[pl.ds(0, 3)], Y_SEND)
    finish(left.at[pl.ds(0, 16)], P_SEND)
    finish(ship, SHIP_SEND)


def widen_kernel(stats, gram, cross, stage, sem):
    fd = stats.shape[4]
    wide, narrow = lax.axis_index("wide"), lax.axis_index("narrow")
    yh, z = wide // NZ, wide % NZ
    yl, x = narrow // (2 * NX), (narrow // 2) % NX
    copies = []
    for src in (0, 1):
        src_yh = yh if src == 0 else 1 - yh
        for slot in range(NZ):
            row = src_yh * NZ + (z + Z_OFFSET[slot] + NZ) % NZ
            for what, (at, dst) in enumerate(((Q_AT, gram), (D_AT, cross))):
                for ly in (0, 1):
                    col_yl = yl if ly == 0 else 1 - yl
                    for xs in range(4):
                        col = col_yl * (2 * NX * fd) + ((x + xs + NX - 1) % NX) * (2 * fd)
                        stage[what, src * NZ + slot, :, pl.ds(pl.multiple_of(col, 2 * fd), 2 * fd)] = stats[
                            src, ly, xs, at[slot]
                        ].astype(F32)
                i = what * 2 * NZ + src * NZ + slot
                c = pltpu.make_async_copy(stage.at[what, src * NZ + slot], dst.at[row, 0], sem.at[i])
                c.start()
                copies.append(c)
    for c in copies:
        c.wait()


def per_device(quantized_inputs, x_full):
    fd, tokens = quantized_inputs.shape
    columns = 16 * fd
    half_out = (2, 4, 16, fd, 2 * fd)
    stats = pl.pallas_call(
        gather_kernel,
        out_shape=pltpu.VMEM((2,) + half_out, BF16),
        in_specs=[pl.BlockSpec(memory_space=pltpu.HBM)] * 2,
        out_specs=pl.BlockSpec(memory_space=pltpu.VMEM),
        scratch_shapes=[
            pltpu.VMEM((16, fd, tokens), BF16),
            pltpu.VMEM((8, fd, tokens), BF16),
            pltpu.VMEM((4, 2, 2, 2, fd, tokens), BF16),
            pltpu.VMEM(half_out, BF16),
            pltpu.SemaphoreType.DMA((5,)),
            pltpu.SemaphoreType.DMA((N_RING,)),
            pltpu.SemaphoreType.DMA((1,)),
            pltpu.SemaphoreType.DMA((3,)),
        ],
        compiler_params=pltpu.CompilerParams(
            collective_id=0, has_side_effects=True, vmem_limit_bytes=(59 * 1024 + 640) * 1024
        ),
    )(quantized_inputs, x_full)
    shape = (16, 1, fd, columns)
    return tuple(
        pl.pallas_call(
            widen_kernel,
            out_shape=[jax.ShapeDtypeStruct(shape, F32)] * 2,
            in_specs=[pl.BlockSpec(memory_space=pltpu.VMEM)],
            out_specs=[pl.BlockSpec(memory_space=pl.ANY)] * 2,
            scratch_shapes=[
                pltpu.VMEM((2, 16, fd, columns), F32),
                pltpu.SemaphoreType.DMA((32,)),
            ],
            compiler_params=pltpu.CompilerParams(vmem_limit_bytes=24 * 2**20),
        )(stats)
    )


def solution(mesh):
    return jax.shard_map(
        per_device,
        mesh=mesh,
        in_specs=(P(("wide", "narrow"), None), P(("wide", "narrow"), None)),
        out_specs=(P(None, "narrow", None, "wide"), P(None, "narrow", None, "wide")),
        check_vma=False,
    )
```

```python
import jax
import jax.numpy as jnp
from jax import lax
from jax.experimental import pallas as pl
from jax.experimental.pallas import tpu as pltpu
from jax.sharding import PartitionSpec as P

MESH = pl.DeviceIdType.MESH
BF16 = jnp.bfloat16
F32 = jnp.float32

NZ, NX = 8, 4
Z_OFFSET = (0, -1, 1, -2, 2, -3, 3, 4)
Q_AT = (0, 2, 3, 6, 7, 10, 11, 14)
D_AT = (1, 4, 5, 8, 9, 12, 13, 15)
OPP, OWN = 0, 1


N_RING = 18 + 6 + 20 + 16
Z_SEND, X_SEND, Y_SEND, P_SEND, SHIP_SEND = range(5)


def gather_kernel(
    q_in, x_in, out, left, xs_left, right, ship, opp_part, own_part, send_sem, ring_sem, out_sem, local_sem
):
    fd, tokens = q_in.shape
    half = fd // 2
    scale = 1.0 / tokens
    wide, narrow = lax.axis_index("wide"), lax.axis_index("narrow")
    yh, z = wide // NZ, wide % NZ
    yl, x, core = narrow // (2 * NX), (narrow // 2) % NX, narrow % 2

    def device(yh_, z_, yl_, x_, core_):
        return (yh_ * NZ + z_, (yl_ * NX + x_) * 2 + core_)

    z_up, z_down = (device(yh, (z + d) % NZ, yl, x, core) for d in (1, NZ - 1))
    x_up, x_down = (device(yh, z, yl, (x + d) % NX, core) for d in (1, NX - 1))
    partner = device(yh, z, yl, x, 1 - core)
    y_opp = device(1 - yh, z, 1 - yl, x, core)
    y_own = device(yh, z, 1 - yl, x, core)

    barrier = pltpu.get_barrier_semaphore()
    y_far = device(1 - yh, z, yl, x, core)
    neighbours = (z_up, z_down, x_up, x_down, partner, y_opp, y_own, y_far)
    for d in neighbours:
        pl.semaphore_signal(barrier, inc=1, device_id=d, device_id_type=MESH)
    pl.semaphore_wait(barrier, len(neighbours))

    ring_count = [0]
    waited = set()

    def copy(src, dst, sender, receive, to):
        return pltpu.make_async_remote_copy(
            src_ref=src,
            dst_ref=dst,
            send_sem=send_sem.at[sender],
            recv_sem=receive,
            device_id=to,
            device_id_type=MESH,
        )

    def make(src, dst, sender, to):
        ring_count[0] += 1
        return copy(src, dst, sender, ring_sem.at[ring_count[0] - 1], to)

    def need(m):
        if id(m) not in waited:
            waited.add(id(m))
            m.wait_recv()

    locals_ = [
        pltpu.make_async_copy(q_in, left.at[0], local_sem.at[0]),
        pltpu.make_async_copy(x_in, xs_left.at[0], local_sem.at[1]),
        pltpu.make_async_copy(q_in, right.at[OWN, 1, 0, core], local_sem.at[2]),
    ]

    lo, hi, rows_all = pl.ds(0, half), pl.ds(half, half), pl.ds(0, fd)
    early, late, all_tokens = pl.ds(0, tokens // 2), pl.ds(tokens // 2, tokens // 2), pl.ds(0, tokens)
    pieces = ((lo, all_tokens), (hi, early), (hi, late))

    z_msgs = {}
    for up in (True, False):
        to = z_up if up else z_down
        for k in (1, 2, 3):
            src, dst = (2 * (k - 1) - 1 if up else 2 * (k - 1)), (2 * k - 1 if up else 2 * k)
            q_src = q_in if k == 1 else left.at[Q_AT[src]]
            x_src = x_in if k == 1 else xs_left.at[src]
            z_msgs[up, k, "q"] = make(q_src, left.at[Q_AT[dst]], Z_SEND, to)
            z_msgs[up, k, "x"] = make(x_src, xs_left.at[dst], Z_SEND, to)
        for i, cut in enumerate(pieces):
            if up:
                z_msgs[up, 4, "q", i] = make(left.at[Q_AT[5], *cut], left.at[Q_AT[7], *cut], Z_SEND, to)
            else:
                z_msgs[up, 4, "x", i] = make(xs_left.at[6, *cut], xs_left.at[7, *cut], Z_SEND, to)

    y_msgs = {}
    for to, hy in ((y_opp, OPP), (y_own, OWN)):
        for h in (lo, hi) if hy == OPP else (hi, lo):
            y_msgs[hy, h is hi] = make(q_in.at[h], right.at[hy, 1, 1, core, h], Y_SEND, to)
    y_two_a = make(right.at[OPP, 1, 1, core, lo], right.at[OPP, 1, 0, core, lo], Y_SEND, y_own)
    y_two_b = make(right.at[OWN, 1, 1, core, hi], right.at[OPP, 1, 0, core, hi], Y_SEND, y_opp)

    x_msgs = {}
    for hy in (OPP, OWN):
        for ly in (0, 1):
            in_halves = (hy, ly) in ((OWN, 0), (OPP, 1))
            for way, slot, to in (("up", 0, x_up), ("down", 2, x_down)):
                x_msgs[way, hy, ly] = []
                for h in (lo, hi) if in_halves else (pl.ds(0, fd),):
                    src = q_in.at[h] if (hy, ly) == (OWN, 0) else right.at[hy, 1, ly, core, h]
                    x_msgs[way, hy, ly].append(make(src, right.at[hy, slot, ly, core, h], X_SEND, to))
            x_msgs["far", hy, ly] = [
                make(right.at[hy, slot, ly, core, h], right.at[hy, 3, ly, core, h], X_SEND, to)
                for slot, h, to in ((0, lo, x_up), (2, hi, x_down))
            ]

    p_msgs = {}
    for xs in range(4):
        for hy in (OPP, OWN):
            for ly in (0, 1):
                src = q_in if (xs, hy, ly) == (1, OWN, 0) else right.at[hy, xs, ly, core]
                p_msgs[xs, hy, ly] = make(src, right.at[hy, xs, ly, core], P_SEND, partner)
    assert ring_count[0] == N_RING, ring_count[0]

    x_way = {0: "up", 2: "down", 3: "far"}

    def right_messages(xs, hy, ly):
        got = [p_msgs[xs, hy, ly]]
        if xs != 1:
            return x_msgs[x_way[xs], hy, ly] + got
        if ly == 0:
            return ([y_two_a, y_two_b] if hy == OPP else []) + got
        return [y_msgs[hy, False], y_msgs[hy, True]] + got

    def block(ref, tile):
        ly, xs, r0, n, h = tile
        if h is None:
            return ref.at[ly, xs, pl.ds(r0, n)]
        return ref.at[ly, xs, pl.ds(r0, n), pl.ds(h * half, half)]

    def ship_out(tile):
        copy(block(ship, tile), block(out.at[1], tile), SHIP_SEND, out_sem.at[0], y_far).start()

    have = set()

    def once(key, fn):
        if key not in have:
            have.add(key)
            fn()

    def subtract(slot, rows, cols):
        left[D_AT[slot], rows, cols] = (
            xs_left[slot, rows, cols].astype(F32) - left[Q_AT[slot], rows, cols].astype(F32)
        ).astype(BF16)

    def left_ready(r0, n, parts=(0, 1, 2)):
        for r in range(r0, r0 + n):
            if r >= 14:
                for i in parts:
                    need(z_msgs[True, 4, "q", i])
                    need(z_msgs[False, 4, "x", i])
                    once(("d", 7, i), lambda i=i: subtract(7, *pieces[i]))
            elif r == 0:
                once("q", locals_[0].wait)
            elif r in Q_AT:
                slot = Q_AT.index(r)
                need(z_msgs[slot % 2 == 1, (slot + 1) // 2, "q"])
            else:
                slot = D_AT.index(r)
                if slot == 0:
                    once("q", locals_[0].wait)
                    once("x", locals_[1].wait)
                else:
                    need(z_msgs[slot % 2 == 1, (slot + 1) // 2, "q"])
                    need(z_msgs[slot % 2 == 1, (slot + 1) // 2, "x"])
                once(("d", slot), lambda slot=slot: subtract(slot, rows_all, all_tokens))

    def right_ready(xs, hy, lys):
        for ly in lys:
            if (xs, hy, ly) == (1, OWN, 0):
                once("r", locals_[2].wait)
            for m in right_messages(xs, hy, ly):
                need(m)

    def dot(hy, xs, nx, lys, r0, n, h=None, cols=None):
        rows = slice(0, fd) if h is None else slice(h * half, (h + 1) * half)
        cols = slice(0, tokens) if cols is None else cols
        a = left[r0 : r0 + n, rows, cols]
        a = a.reshape(-1, a.shape[-1])
        b = right[hy, xs : xs + nx, lys[0] : lys[-1] + 1, :, :, cols]
        b = b.reshape(-1, b.shape[-1])
        return lax.dot_general(a, b, (((1,), (1,)), ((), ())), preferred_element_type=F32)

    def rounded(p, n):
        return (p * scale).astype(BF16).reshape(n, p.shape[0] // n, p.shape[1])

    def put_own(p, r0, n, xs, nx):
        p = rounded(p, n)
        for i in range(nx):
            for ly in (0, 1):
                at = (2 * i + ly) * 2 * fd
                out[0, ly, xs + i, r0 : r0 + n] = p[..., at : at + 2 * fd]

    def put_ship(p, r0, n, xs, nx, lys, h):
        p = rounded(p, n)
        rows = slice(0, fd) if h is None else slice(h * half, (h + 1) * half)
        for i in range(nx):
            for j, ly in enumerate(lys):
                at = (len(lys) * i + j) * 2 * fd
                ship[ly, xs + i, r0 : r0 + n, rows] = p[..., at : at + 2 * fd]

    events = []

    def at(time, fn):
        events.append((time, len(events), fn))

    def forward_z(what, k):
        def go():
            for up in (True, False):
                need(z_msgs[up, k, what])
                if k < 3:
                    z_msgs[up, k + 1, what].start()
                elif up == (what == "q"):
                    for i in range(3):
                        z_msgs[up, 4, what, i].start()

        return go

    for k in (1, 2, 3):
        at(2 * k - 1 + 0.05, forward_z("q", k))
        at(2 * k + 0.05, forward_z("x", k))

    def start_all():
        for key in ((True, 1, "q"), (False, 1, "q")):
            z_msgs[key].start()
        for m in y_msgs.values():
            m.start()
        x_msgs["up", OWN, 0][0].start()
        x_msgs["down", OWN, 0][0].start()
        p_msgs[1, OWN, 0].start()
        for key in ((True, 1, "x"), (False, 1, "x")):
            z_msgs[key].start()
        for c in locals_:
            c.start()

    at(0.0, start_all)

    def to_x(hy, ly, i=0):
        x_msgs["up", hy, ly][i].start()
        x_msgs["down", hy, ly][i].start()

    def y_first_half():
        need(y_msgs[OPP, False])
        y_two_a.start()
        to_x(OPP, 1, 0)
        need(y_msgs[OWN, True])
        y_two_b.start()

    at(0.55, y_first_half)

    def y_second_half():
        need(y_msgs[OPP, True])
        to_x(OPP, 1, 1)
        p_msgs[1, OPP, 1].start()
        need(y_msgs[OWN, False])
        p_msgs[1, OWN, 1].start()

    at(1.04, y_second_half)

    def y_two_arrived():
        need(y_two_a)
        need(y_two_b)
        to_x(OPP, 0)
        p_msgs[1, OPP, 0].start()

    at(1.6, y_two_arrived)

    def x_arrived(hy, ly):
        def go():
            for i, way in enumerate(("up", "down")):
                for m in x_msgs[way, hy, ly]:
                    need(m)
                x_msgs["far", hy, ly][i].start()
                p_msgs[2 * i, hy, ly].start()

        return go

    at(1.65, x_arrived(OPP, 1))
    at(2.70, x_arrived(OPP, 0))
    at(2.71, lambda: to_x(OWN, 0, 1))
    at(4.20, x_arrived(OWN, 0))
    at(5.20, x_arrived(OWN, 1))

    def far_arrived(hy, ly):
        def go():
            for m in x_msgs["far", hy, ly]:
                need(m)
            p_msgs[3, hy, ly].start()

        return go

    at(3.18, far_arrived(OPP, 1))
    at(3.19, lambda: to_x(OWN, 1))
    at(3.70, far_arrived(OPP, 0))
    at(5.70, far_arrived(OWN, 0))
    at(6.22, far_arrived(OWN, 1))

    pending = []

    def flush():
        while pending:
            ship_out(pending.pop(0))

    def opp_at(time, r0, n, xs, nx=1, lys=(0, 1), h=None):
        def go():
            left_ready(r0, n, (0, 1, 2) if h is None else (h,))
            for i in range(nx):
                right_ready(xs + i, OPP, lys)
            before = list(pending)
            put_ship(dot(OPP, xs, nx, lys, r0, n, h), r0, n, xs, nx, lys, h)
            if before:
                flush()
            pending.extend((ly, xs + i, r0, n, h) for i in range(nx) for ly in lys)

        at(time, go)

    def own_at(time, r0, n, xs, nx=1):
        def go():
            left_ready(r0, n)
            for i in range(nx):
                right_ready(xs + i, OWN, (0, 1))
            put_own(dot(OWN, xs, nx, (0, 1), r0, n), r0, n, xs, nx)
            flush()

        at(time, go)

    def last_early():
        left_ready(14, 2, (0, 1))
        cols = slice(0, tokens // 2)
        for xs in (0, 2):
            span = slice(xs * 4 * fd, (xs + 2) * 4 * fd)
            opp_part[:, span] = dot(OPP, xs, 2, (0, 1), 14, 2, 1, cols)
        flush()
        for xs in (0, 2):
            for i in (0, 1):
                right_ready(xs + i, OWN, (0, 1))
            span = slice(xs * 4 * fd, (xs + 2) * 4 * fd)
            own_part[:, span] = dot(OWN, xs, 2, (0, 1), 12, 4, None, cols)

    def last_late():
        left_ready(14, 2)
        cols = slice(tokens // 2, tokens)
        for xs in (0, 2):
            span = slice(xs * 4 * fd, (xs + 2) * 4 * fd)
            p = opp_part[:, span] + dot(OPP, xs, 2, (0, 1), 14, 2, 1, cols)
            put_ship(p, 14, 2, xs, 2, (0, 1), 1)
            flush()
            pending.extend((ly, xs + i, 14, 2, 1) for i in (0, 1) for ly in (0, 1))
        for xs in (0, 2):
            span = slice(xs * 4 * fd, (xs + 2) * 4 * fd)
            p = own_part[:, span] + dot(OWN, xs, 2, (0, 1), 12, 4, None, cols)
            put_own(p, 12, 4, xs, 2)
            flush()

    opp_at(1.25, 0, 4, 1, 1, (1,))
    own_at(1.35, 0, 4, 1)
    opp_at(1.72, 0, 4, 1, 1, (0,))
    for i, xs in enumerate((0, 2)):
        opp_at(1.80 + 0.08 * i, 0, 4, xs, 1, (1,))
    opp_at(2.10, 4, 2, 1)
    for i, xs in enumerate((0, 2)):
        opp_at(2.18 + 0.08 * i, 4, 2, xs, 1, (1,))
    for i, xs in enumerate((0, 2)):
        opp_at(2.82 + 0.10 * i, 0, 6, xs, 1, (0,))
    opp_at(3.10, 6, 2, 0, 2)
    opp_at(3.17, 6, 2, 2)
    opp_at(3.35, 0, 8, 3, 1, (1,))
    opp_at(3.85, 0, 8, 3, 1, (0,))
    own_at(3.95, 4, 4, 1)
    for i, xs in enumerate((0, 2)):
        opp_at(4.10 + 0.15 * i, 8, 2, xs, 2)
        opp_at(5.10 + 0.15 * i, 10, 2, xs, 2)
        opp_at(6.10 + 0.15 * i, 12, 2, xs, 2)
        opp_at(6.60 + 0.12 * i, 14, 2, xs, 2, (0, 1), 0)
    own_at(5.42, 0, 8, 0)
    own_at(5.55, 0, 8, 2)
    own_at(5.76, 8, 4, 0, 2)
    own_at(6.43, 0, 8, 3)
    at(6.85, last_early)
    at(7.05, last_late)
    own_at(7.30, 8, 4, 2, 2)

    for _, _, fn in sorted(events, key=lambda e: e[:2]):
        fn()

    def finish(ref, sender):
        copy(ref, ref, sender, out_sem.at[0], z_up).wait_send()

    copy(out.at[1], out.at[1], SHIP_SEND, out_sem.at[0], z_up).wait_recv()
    finish(left.at[pl.ds(0, 14)], Z_SEND)
    finish(left.at[pl.ds(0, 12)], X_SEND)
    finish(left.at[pl.ds(0, 3)], Y_SEND)
    finish(left.at[pl.ds(0, 16)], P_SEND)
    finish(ship, SHIP_SEND)


def widen_kernel(stats, gram, cross, stage, sem):
    fd = stats.shape[4]
    wide, narrow = lax.axis_index("wide"), lax.axis_index("narrow")
    yh, z = wide // NZ, wide % NZ
    yl, x = narrow // (2 * NX), (narrow // 2) % NX
    copies = []
    for src in (0, 1):
        src_yh = yh if src == 0 else 1 - yh
        for slot in range(NZ):
            row = src_yh * NZ + (z + Z_OFFSET[slot] + NZ) % NZ
            for what, (at, dst) in enumerate(((Q_AT, gram), (D_AT, cross))):
                for ly in (0, 1):
                    col_yl = yl if ly == 0 else 1 - yl
                    for xs in range(4):
                        col = col_yl * (2 * NX * fd) + ((x + xs + NX - 1) % NX) * (2 * fd)
                        stage[what, src * NZ + slot, :, pl.ds(pl.multiple_of(col, 2 * fd), 2 * fd)] = stats[
                            src, ly, xs, at[slot]
                        ].astype(F32)
                i = what * 2 * NZ + src * NZ + slot
                c = pltpu.make_async_copy(stage.at[what, src * NZ + slot], dst.at[row, 0], sem.at[i])
                c.start()
                copies.append(c)
    for c in copies:
        c.wait()


def per_device(quantized_inputs, x_full):
    fd, tokens = quantized_inputs.shape
    columns = 16 * fd
    half_out = (2, 4, 16, fd, 2 * fd)
    stats = pl.pallas_call(
        gather_kernel,
        out_shape=pltpu.VMEM((2,) + half_out, BF16),
        in_specs=[pl.BlockSpec(memory_space=pltpu.HBM)] * 2,
        out_specs=pl.BlockSpec(memory_space=pltpu.VMEM),
        scratch_shapes=[
            pltpu.VMEM((16, fd, tokens), BF16),
            pltpu.VMEM((8, fd, tokens), BF16),
            pltpu.VMEM((2, 4, 2, 2, fd, tokens), BF16),
            pltpu.VMEM(half_out, BF16),
            pltpu.VMEM((fd, columns), F32),
            pltpu.VMEM((4 * fd, columns), F32),
            pltpu.SemaphoreType.DMA((5,)),
            pltpu.SemaphoreType.DMA((N_RING,)),
            pltpu.SemaphoreType.DMA((1,)),
            pltpu.SemaphoreType.DMA((3,)),
        ],
        compiler_params=pltpu.CompilerParams(
            collective_id=0, has_side_effects=True, vmem_limit_bytes=(59 * 1024 + 640) * 1024
        ),
    )(quantized_inputs, x_full)
    shape = (16, 1, fd, columns)
    return tuple(
        pl.pallas_call(
            widen_kernel,
            out_shape=[jax.ShapeDtypeStruct(shape, F32)] * 2,
            in_specs=[pl.BlockSpec(memory_space=pltpu.VMEM)],
            out_specs=[pl.BlockSpec(memory_space=pl.ANY)] * 2,
            scratch_shapes=[
                pltpu.VMEM((2, 16, fd, columns), F32),
                pltpu.SemaphoreType.DMA((32,)),
            ],
            compiler_params=pltpu.CompilerParams(vmem_limit_bytes=24 * 2**20),
        )(stats)
    )


def solution(mesh):
    return jax.shard_map(
        per_device,
        mesh=mesh,
        in_specs=(P(("wide", "narrow"), None), P(("wide", "narrow"), None)),
        out_specs=(P(None, "narrow", None, "wide"), P(None, "narrow", None, "wide")),
        check_vma=False,
    )
```
